32 devices in a mesh: dp: 8 (over y, x, core), tensor: 4 (over z).
Axes of the slice: x: 2, y: 2, z: 4, core: 2. Of those that a mesh axis runs over, the one named last changes fastest.
Arguments:
- tokens: bfloat16 [4608, 1024], P('dp', 'tensor'), may hold values from -6 to 6
- first_gain: float32 [2, 1024], replicated, may hold values from 0.25 to 1.75
- first_bias: float32 [2, 1024], replicated, may hold values from -1.75 to 1.75
- triple_weight: bfloat16 [2, 1024, 3072], P(None, None, 'tensor'), as said below
- query_bias: float32 [2, 1024], P(None, 'tensor'), may hold values from -3 to 3
- value_bias: float32 [2, 1024], P(None, 'tensor'), may hold values from -3 to 3
- output_weight: bfloat16 [2, 1024, 1024], P(None, 'tensor'), may hold values from -0.375 to 0.375
- output_bias: float32 [2, 1024], replicated, may hold values from -1.75 to 1.75
- second_gain: float32 [2, 1024], replicated, may hold values from 0.25 to 1.75
- second_bias: float32 [2, 1024], replicated, may hold values from -1.75 to 1.75
- up_weight: bfloat16 [2, 1024, 4096], P(None, None, 'tensor'), may hold values from -0.1875 to 0.1875
- up_bias: float32 [2, 4096], P(None, 'tensor'), may hold values from -3 to 3
- down_weight: bfloat16 [2, 4096, 1024], P(None, 'tensor'), may hold values from -0.125 to 0.125
- down_bias: float32 [2, 1024], replicated, may hold values from -1.75 to 1.75
- cotangent: bfloat16 [4608, 1024], P('dp', 'tensor'), may hold values from -6 to 6
Outputs:
- block_out: float32 [4608, 1024], P('dp', 'tensor')
- grad_tokens: float32 [4608, 1024], P('dp', 'tensor')
- grad_first_gain: float32 [2, 1024], replicated
- grad_first_bias: float32 [2, 1024], replicated
- grad_triple: float32 [2, 1024, 3072], P(None, None, 'tensor')
- grad_query_bias: float32 [2, 1024], P(None, 'tensor')
- grad_value_bias: float32 [2, 1024], P(None, 'tensor')
- grad_output_weight: float32 [2, 1024, 1024], P(None, 'tensor')
- grad_output_bias: float32 [2, 1024], replicated
- grad_second_gain: float32 [2, 1024], replicated
- grad_second_bias: float32 [2, 1024], replicated
- grad_up: float32 [2, 1024, 4096], P(None, None, 'tensor')
- grad_up_bias: float32 [2, 4096], P(None, 'tensor')
- grad_down: float32 [2, 4096, 1024], P(None, 'tensor')
- grad_down_bias: float32 [2, 1024], replicated
The draws below stay inside these ranges and needn't reach their ends.
Inputs may be any that keep to these rules, and one draw needn't show every extreme that they name: `triple_weight`: columns ordered by head, then query, key, value, then the head's 64 entries.
All inputs are finite; a program needn't handle non-finite values.
Results may differ from the reference program's by a relative error of at most 0.025.
Values may be sent and summed in bfloat16 or wider, within the bound.
No kernel may reach another device: no remote copies, remote signals or barrier semaphores. Data moves between devices by JAX's collectives and lax.ppermute only.
A program may use at most 192 MiB of HBM per device.

```python
import jax
import jax.numpy as jnp
from jax import lax

D = 1024
HEADS = 16
HEAD = 64
FF = 4096
LAYERS = 2
LEN = 576
TOKENS = 4608


def draw_triple_weight(key, part):
    base = jnp.clip(jax.random.normal(key, (LAYERS, D, HEADS, 3, HEAD), jnp.float32), -6.0, 6.0) * D ** (-0.5)
    return base.reshape(LAYERS, D, 3 * D).astype(jnp.bfloat16)


def block_scale(stream_key, shape, split, low, top_value):
    level, own = 1.0, jax.random.fold_in(stream_key, 6)
    for dim, parts in split:
        steps = jnp.exp(jax.random.uniform(jax.random.fold_in(own, dim), (parts,), jnp.float32, low / len(split), top_value / len(split)))
        level = level * jnp.repeat(steps, shape[dim] // parts).reshape([-1 if axis == dim else 1 for axis in range(len(shape))])
    return level


def bell_draw(own_key, extent, deviation, limit, cuts=(), held_as=jnp.bfloat16):
    drawn = jax.random.normal(own_key, extent, jnp.float32) * deviation
    if len(cuts) > 0:
        drawn = block_scale(own_key, extent, cuts, -0.22, 0.18) * drawn
    return jnp.clip(drawn, min=-limit, max=limit).astype(held_as)


def setup_inputs(seed: int = 0) -> dict:
    streams_of = jax.random.split(jax.random.key(seed), 16)
    tokens = bell_draw(streams_of[0], (TOKENS, D), 1.0, 6.0, ((0, 8), (1, 4)))
    first_gain = jnp.clip(1.0 + 0.15 * jax.random.normal(streams_of[1], (LAYERS, D), jnp.float32), 0.25, 1.75)
    first_bias = bell_draw(streams_of[2], (LAYERS, D), 0.3, 1.75, (), jnp.float32)
    triple_weight = draw_triple_weight(jax.random.fold_in(streams_of[15], 71), 0)
    query_bias = bell_draw(streams_of[4], (LAYERS, D), 0.5, 3.0, ((1, 4),), jnp.float32)
    value_bias = bell_draw(streams_of[5], (LAYERS, D), 0.5, 3.0, ((1, 4),), jnp.float32)
    output_weight = bell_draw(streams_of[6], (LAYERS, D, D), (D // 4) ** -0.5, 0.375, ((1, 4),))
    output_bias = bell_draw(streams_of[7], (LAYERS, D), 0.3, 1.75, (), jnp.float32)
    second_gain = jnp.clip(1.0 + 0.15 * jax.random.normal(streams_of[8], (LAYERS, D), jnp.float32), 0.25, 1.75)
    second_bias = bell_draw(streams_of[9], (LAYERS, D), 0.3, 1.75, (), jnp.float32)
    up_weight = bell_draw(streams_of[10], (LAYERS, D, FF), D ** -0.5, 0.1875, ((2, 4),))
    up_bias = bell_draw(streams_of[11], (LAYERS, FF), 0.5, 3.0, ((1, 4),), jnp.float32)
    down_weight = bell_draw(streams_of[12], (LAYERS, FF, D), (FF // 2) ** -0.5, 0.125, ((1, 4),))
    down_bias = bell_draw(streams_of[13], (LAYERS, D), 0.3, 1.75, (), jnp.float32)
    cotangent = bell_draw(streams_of[14], (TOKENS, D), 1.0, 6.0, ((0, 8), (1, 4)))
    return dict(tokens=tokens, first_gain=first_gain, first_bias=first_bias, triple_weight=triple_weight, query_bias=query_bias, value_bias=value_bias, output_weight=output_weight, output_bias=output_bias, second_gain=second_gain, second_bias=second_bias, up_weight=up_weight, up_bias=up_bias, down_weight=down_weight, down_bias=down_bias, cotangent=cotangent)


EPS = 1e-05
CUBIC = 0.044715
ROOT = 0.7978845608028654

def activate(inputs):
    return 0.5 * inputs * (1.0 + jnp.tanh(ROOT * (inputs + CUBIC * inputs * inputs * inputs)))

def activate_grad(inputs, upstream):
    return jax.vjp(activate, inputs)[1](upstream)[0]

def contract_rows(former, latter):
    return lax.dot_general(former, latter, (((0,), (0,)), ((), ())), preferred_element_type=jnp.float32)

def contract_cols(former, latter):
    return lax.dot_general(former, latter, (((1,), (1,)), ((), ())), preferred_element_type=jnp.float32)

def alibi_scores(queries, key_part):
    length = queries.shape[1]
    head_ids = jnp.arange(HEADS).astype(jnp.float32)
    slopes = jnp.exp2(-8.0 * (head_ids + 1.0) / HEADS)
    position = jnp.arange(length)
    distance = (position[:, None] - position[None, :]).astype(jnp.float32)
    scores = jnp.einsum('sqhd,skhd->shqk', queries.astype(jnp.float32), key_part.astype(jnp.float32)) * HEAD ** (-0.5)
    scores = scores - slopes[None, :, None, None] * distance[None, None]
    return jnp.where((distance >= 0)[None, None], scores, -jnp.inf)

def attend_forward(queries, key_part, values):
    scores = alibi_scores(queries, key_part)
    highest = lax.optimization_barrier(jnp.max(scores, -1, keepdims=True))
    log_total = highest + jnp.log(lax.optimization_barrier(jnp.sum(jnp.exp(scores - highest), -1, keepdims=True)))
    attention = jnp.exp(scores - log_total).astype(jnp.bfloat16)
    context = jnp.einsum('shqk,skhd->sqhd', attention.astype(jnp.float32), values.astype(jnp.float32))
    return (context.astype(jnp.bfloat16), log_total)

def attend_backward(queries, key_part, values, log_total, grad_context):
    attention = jnp.exp(alibi_scores(queries, key_part) - log_total)
    rounded = attention.astype(jnp.bfloat16).astype(jnp.float32)
    context_f = grad_context.astype(jnp.float32)
    grad_values = jnp.einsum('shqk,sqhd->skhd', rounded, context_f)
    grad_attention = jnp.einsum('sqhd,skhd->shqk', context_f, values.astype(jnp.float32))
    grad_scores = attention * (grad_attention - lax.optimization_barrier(jnp.sum(attention * grad_attention, -1, keepdims=True)))
    score_half = (grad_scores * HEAD ** (-0.5)).astype(jnp.bfloat16).astype(jnp.float32)
    grad_queries = jnp.einsum('shqk,skhd->sqhd', score_half, key_part.astype(jnp.float32))
    grad_keys = jnp.einsum('shqk,sqhd->skhd', score_half, queries.astype(jnp.float32))
    return (grad_queries, grad_keys, grad_values)

def norm_forward(stream, gain, bias):
    average = lax.optimization_barrier(jnp.mean(stream, 1, keepdims=True))
    centred = stream - average
    reciprocal = lax.rsqrt(lax.optimization_barrier(jnp.mean(centred * centred, 1, keepdims=True)) + EPS)
    normed = centred * reciprocal
    return ((normed * gain + bias).astype(jnp.bfloat16), normed, reciprocal)

def norm_backward(grad_normed, normed, reciprocal, gain):
    scaled = grad_normed * gain
    first_mean = lax.optimization_barrier(jnp.mean(scaled, 1, keepdims=True))
    second_mean = lax.optimization_barrier(jnp.mean(scaled * normed, 1, keepdims=True))
    result = reciprocal * (scaled - first_mean - normed * second_mean)
    return (result, lax.optimization_barrier(jnp.sum(grad_normed * normed, 0)), lax.optimization_barrier(jnp.sum(grad_normed, 0)))

def run_attention(queries, key_part, values):
    sequences = queries.shape[0] // LEN

    def one_sequence(pieces):
        context, log_total = attend_forward(pieces[0][None], pieces[1][None], pieces[2][None])
        return (context[0], log_total[0])
    shaped = (queries.reshape(sequences, LEN, HEADS, HEAD), key_part.reshape(sequences, LEN, HEADS, HEAD), values.reshape(sequences, LEN, HEADS, HEAD))
    return lax.map(one_sequence, shaped)

def run_attention_back(queries, key_part, values, log_total, grad_context):
    sequences = queries.shape[0] // LEN

    def one_sequence(pieces):
        grads = attend_backward(pieces[0][None], pieces[1][None], pieces[2][None], pieces[3][None], pieces[4][None])
        return (grads[0][0], grads[1][0], grads[2][0])
    shaped = (queries.reshape(sequences, LEN, HEADS, HEAD), key_part.reshape(sequences, LEN, HEADS, HEAD), values.reshape(sequences, LEN, HEADS, HEAD), log_total, grad_context.reshape(sequences, LEN, HEADS, HEAD))
    return lax.map(one_sequence, shaped)

def reference(tokens, first_gain, first_bias, triple_weight, query_bias, value_bias, output_weight, output_bias, second_gain, second_bias, up_weight, up_bias, down_weight, down_bias, cotangent):
    count = tokens.shape[0]
    stream = tokens.astype(jnp.float32)
    stored_all = []
    for layer_index in range(LAYERS):
        first_rows, first_normed, first_recip = norm_forward(stream, first_gain[layer_index], first_bias[layer_index])
        projected = jnp.dot(first_rows, triple_weight[layer_index], preferred_element_type=jnp.float32).reshape(count, HEADS, 3, HEAD)
        queries = (projected[:, :, 0] + query_bias[layer_index].reshape(HEADS, HEAD)).astype(jnp.bfloat16)
        key_part = projected[:, :, 1].astype(jnp.bfloat16)
        values = (projected[:, :, 2] + value_bias[layer_index].reshape(HEADS, HEAD)).astype(jnp.bfloat16)
        context, log_total = run_attention(queries, key_part, values)
        context_rows = context.reshape(count, D)
        branch = jnp.dot(context_rows, output_weight[layer_index], preferred_element_type=jnp.float32) + output_bias[layer_index]
        stream = stream + branch
        second_rows, second_normed, second_recip = norm_forward(stream, second_gain[layer_index], second_bias[layer_index])
        pre_act = jnp.dot(second_rows, up_weight[layer_index], preferred_element_type=jnp.float32) + up_bias[layer_index]
        hidden = activate(pre_act).astype(jnp.bfloat16)
        branch = jnp.dot(hidden, down_weight[layer_index], preferred_element_type=jnp.float32) + down_bias[layer_index]
        stream = stream + branch
        stored_all.append((first_rows, first_normed, first_recip, queries, key_part, values, log_total, context_rows, second_rows, second_normed, second_recip, pre_act, hidden))
    block_out = stream
    gradient = cotangent.astype(jnp.float32)
    results = [None] * LAYERS
    for layer_index in reversed(range(LAYERS)):
        first_rows, first_normed, first_recip, queries, key_part, values, log_total, context_rows, second_rows, second_normed, second_recip, pre_act, hidden = stored_all[layer_index]
        grad_down_bias = lax.optimization_barrier(jnp.sum(gradient, 0))
        grad_rows = gradient.astype(jnp.bfloat16)
        grad_down = contract_rows(hidden, grad_rows)
        grad_hidden = contract_cols(grad_rows, down_weight[layer_index])
        grad_pre = activate_grad(pre_act, grad_hidden)
        pre_half = grad_pre.astype(jnp.bfloat16)
        grad_up = contract_rows(second_rows, pre_half)
        grad_up_bias = lax.optimization_barrier(jnp.sum(grad_pre, 0))
        grad_second = contract_cols(pre_half, up_weight[layer_index])
        step_grad, grad_second_gain, grad_second_bias = norm_backward(grad_second, second_normed, second_recip, second_gain[layer_index])
        gradient = gradient + step_grad
        grad_output_bias = lax.optimization_barrier(jnp.sum(gradient, 0))
        grad_rows = gradient.astype(jnp.bfloat16)
        grad_output = contract_rows(context_rows, grad_rows)
        grad_context = contract_cols(grad_rows, output_weight[layer_index]).astype(jnp.bfloat16)
        grad_queries, grad_keys, grad_values = run_attention_back(queries, key_part, values, log_total, grad_context)
        grad_queries = grad_queries.reshape(count, HEADS, HEAD)
        grad_keys = grad_keys.reshape(count, HEADS, HEAD)
        grad_values = grad_values.reshape(count, HEADS, HEAD)
        grad_query_bias = lax.optimization_barrier(jnp.sum(grad_queries, 0)).reshape(D)
        grad_value_bias = lax.optimization_barrier(jnp.sum(grad_values, 0)).reshape(D)
        grad_joined = jnp.stack([grad_queries, grad_keys, grad_values], axis=2).reshape(count, 3 * D).astype(jnp.bfloat16)
        grad_triple = contract_rows(first_rows, grad_joined)
        grad_first = contract_cols(grad_joined, triple_weight[layer_index])
        step_grad, grad_first_gain, grad_first_bias = norm_backward(grad_first, first_normed, first_recip, first_gain[layer_index])
        gradient = gradient + step_grad
        results[layer_index] = (grad_first_gain, grad_first_bias, grad_triple, grad_query_bias, grad_value_bias, grad_output, grad_output_bias, grad_second_gain, grad_second_bias, grad_up, grad_up_bias, grad_down, grad_down_bias)
    stacked = [jnp.stack([results[source][member] for source in range(LAYERS)]) for member in range(13)]
    return (block_out, gradient, stacked[0], stacked[1], stacked[2], stacked[3], stacked[4], stacked[5], stacked[6], stacked[7], stacked[8], stacked[9], stacked[10], stacked[11], stacked[12])
```

```python
import functools

import jax
import jax.numpy as jnp
from jax import lax
from jax.experimental import pallas as pl
from jax.experimental.pallas import tpu as pltpu
from jax.sharding import Mesh, PartitionSpec as P

HEAD = 64
LAYERS = 2

EPS = 1e-05
CUBIC = 0.044715
ROOT = 0.7978845608028654
LOW = -1e30

HALF = jnp.bfloat16
FULL = jnp.float32


def activate(inputs):
    return 0.5 * inputs * (1.0 + jnp.tanh(ROOT * (inputs + CUBIC * inputs * inputs * inputs)))


def activate_grad(inputs, upstream):
    return jax.vjp(activate, inputs)[1](upstream)[0]


def dot(former, latter, former_dim, latter_dim):
    return lax.dot_general(
        former, latter, (((former_dim,), (latter_dim,)), ((), ())), preferred_element_type=FULL
    )


def softmax_rows(queries, key_part, slope, distance):
    scores = dot(queries, key_part, 1, 1) * HEAD ** (-0.5) - slope * distance
    scores = jnp.where(distance >= 0, scores, LOW)
    raised = jnp.exp(scores - jnp.max(scores, -1, keepdims=True))
    return raised * (1.0 / jnp.sum(raised, -1, keepdims=True))


def forward_kernel(pieces, slope_ref, column_ref, row_ref, joined_ref, context_ref):
    length = joined_ref.shape[0]
    rows = length // pieces
    pair = pl.program_id(0)
    for member in range(2):
        slope = slope_ref[2 * pair + member]
        start = member * 3 * HEAD
        key_part = joined_ref[:, start + HEAD : start + 2 * HEAD]
        values = joined_ref[:, start + 2 * HEAD : start + 3 * HEAD]
        for piece in range(pieces):
            span = slice(piece * rows, (piece + 1) * rows)
            distance = column_ref[span, :] - row_ref[...]
            attention = softmax_rows(
                joined_ref[span, start : start + HEAD], key_part, slope, distance
            )
            context = dot(attention.astype(HALF), values, 1, 0)
            context_ref[span, member * HEAD : (member + 1) * HEAD] = context.astype(HALF)


def backward_kernel(
    pieces,
    slope_ref,
    column_ref,
    row_ref,
    joined_ref,
    context_ref,
    grad_ref,
    total_ref,
    key_ref,
    value_ref,
):
    length = joined_ref.shape[0]
    rows = length // pieces
    pair = pl.program_id(0)
    for member in range(2):
        slope = slope_ref[2 * pair + member]
        start = member * 3 * HEAD
        key_part = joined_ref[:, start + HEAD : start + 2 * HEAD]
        values = joined_ref[:, start + 2 * HEAD : start + 3 * HEAD]
        query_total = jnp.zeros((1, HEAD), FULL)
        for piece in range(pieces):
            span = slice(piece * rows, (piece + 1) * rows)
            distance = column_ref[span, :] - row_ref[...]
            queries = joined_ref[span, start : start + HEAD]
            upstream = context_ref[span, member * HEAD : (member + 1) * HEAD]
            attention = softmax_rows(queries, key_part, slope, distance)
            grad_values = dot(attention.astype(HALF), upstream, 0, 0)
            grad_attention = dot(upstream, values, 1, 1)
            weighted = attention * grad_attention
            grad_scores = weighted - attention * jnp.sum(weighted, -1, keepdims=True)
            score_half = (grad_scores * HEAD ** (-0.5)).astype(HALF)
            grad_queries = dot(score_half, key_part, 1, 0)
            grad_keys = dot(score_half, queries, 0, 0)
            grad_ref[span, start : start + HEAD] = grad_queries.astype(HALF)
            query_total = query_total + jnp.sum(grad_queries, 0, keepdims=True)
            if piece == 0:
                key_ref[...] = grad_keys
                value_ref[...] = grad_values
            else:
                key_ref[...] += grad_keys
                value_ref[...] += grad_values
        grad_ref[:, start + HEAD : start + 2 * HEAD] = key_ref[...].astype(HALF)
        grad_ref[:, start + 2 * HEAD : start + 3 * HEAD] = value_ref[...].astype(HALF)
        eight = (8, HEAD)
        total_ref[0, :, start : start + HEAD] = jnp.broadcast_to(query_total, eight)
        total_ref[0, :, start + HEAD : start + 2 * HEAD] = jnp.zeros(eight, FULL)
        total_ref[0, :, start + 2 * HEAD : start + 3 * HEAD] = jnp.broadcast_to(
            jnp.sum(value_ref[...], 0, keepdims=True), eight
        )


def attention_specs(length):
    return [
        pl.BlockSpec(memory_space=pltpu.SMEM),
        pl.BlockSpec((length, 1), lambda pair: (0, 0)),
        pl.BlockSpec((1, length), lambda pair: (0, 0)),
        pl.BlockSpec((length, 6 * HEAD), lambda pair: (0, pair)),
    ]


def attend_forward(joined, slopes, place):
    length, width = joined.shape
    pairs = width // (6 * HEAD)
    return pl.pallas_call(
        functools.partial(forward_kernel, 4),
        name="attend_forward",
        grid=(pairs,),
        in_specs=attention_specs(length),
        out_specs=pl.BlockSpec((length, 2 * HEAD), lambda pair: (0, pair)),
        out_shape=jax.ShapeDtypeStruct((length, pairs * 2 * HEAD), HALF),
        cost_estimate=pl.CostEstimate(
            flops=pairs * 2 * 4 * length * length * HEAD,
            bytes_accessed=length * width * 3,
            transcendentals=pairs * 2 * length * length,
        ),
    )(slopes, place[:, None], place[None, :], joined)


def attend_backward(joined, grad_context, slopes, place):
    length, width = joined.shape
    pairs = width // (6 * HEAD)
    grad_joined, totals = pl.pallas_call(
        functools.partial(backward_kernel, 4),
        name="attend_backward",
        grid=(pairs,),
        in_specs=attention_specs(length)
        + [pl.BlockSpec((length, 2 * HEAD), lambda pair: (0, pair))],
        out_specs=[
            pl.BlockSpec((length, 6 * HEAD), lambda pair: (0, pair)),
            pl.BlockSpec((1, 8, 6 * HEAD), lambda pair: (pair, 0, 0)),
        ],
        out_shape=[
            jax.ShapeDtypeStruct((length, width), HALF),
            jax.ShapeDtypeStruct((pairs, 8, 6 * HEAD), FULL),
        ],
        scratch_shapes=[pltpu.VMEM((length, HEAD), FULL), pltpu.VMEM((length, HEAD), FULL)],
        cost_estimate=pl.CostEstimate(
            flops=pairs * 2 * 10 * length * length * HEAD,
            bytes_accessed=length * width * 5,
            transcendentals=pairs * 2 * length * length,
        ),
    )(slopes, place[:, None], place[None, :], joined, grad_context)
    return grad_joined, totals[:, 0].reshape(width)


def xor_pairs(count, bit):
    return [(source, source ^ bit) for source in range(count)]


def other_core(block):
    return lax.ppermute(block, "c", [(0, 1), (1, 0)])


def is_home():
    return lax.axis_index("c") == lax.axis_index("h")


def trade(block):
    received = lax.ppermute(block, ("c", "h"), [(1, 2), (2, 1)])
    return jnp.where(is_home(), block, received)


def group_index():
    return lax.axis_index("c") * lax.axis_size("r") + lax.axis_index("r")


def xor_order(blocks, index):
    bit = 1
    while bit < len(blocks):
        flip = (index // bit) % 2 == 1
        blocks = [
            jnp.where(flip, blocks[slot ^ bit], blocks[slot]) for slot in range(len(blocks))
        ]
        bit *= 2
    return blocks


def gather_list(own):
    ring = lax.axis_size("r")
    near = {0: own}
    bit = 1
    while bit < ring:
        for slot in list(near):
            near[slot ^ bit] = lax.ppermute(near[slot], "r", xor_pairs(ring, bit))
        bit *= 2
    near = [near[slot] for slot in range(ring)]
    return near + [other_core(block) for block in near]


def gather_rows(own):
    return jnp.concatenate(gather_list(own), 0)


def scatter_rows(partial_value):
    ring = lax.axis_size("r")
    half = partial_value.shape[0] // 2
    block = half // ring
    total = partial_value[:half].astype(FULL) + other_core(partial_value[half:]).astype(FULL)
    count = ring
    while count > 1:
        bit = count // 2
        sent = lax.ppermute(
            total[bit * block :].astype(HALF), "r", xor_pairs(ring, bit)
        )
        total = total[: bit * block] + sent.astype(FULL)
        count = bit
    return total


def enter(shard):
    index = group_index()
    blocks = gather_list(trade(shard))
    full = jnp.concatenate(xor_order(blocks, index), 1)
    count = len(blocks)
    rows = full.shape[0] // count
    parts = [full[slot * rows : (slot + 1) * rows] for slot in range(count)]
    return jnp.concatenate(xor_order(parts, index), 0)


def leave(own):
    index = group_index()
    count = 2 * lax.axis_size("r")
    width = own.shape[1] // count
    own = own.astype(HALF)
    parts = xor_order([own[:, slot * width : (slot + 1) * width] for slot in range(count)], index)
    parts = [parts[0]] + [
        lax.ppermute(parts[slot], ("c", "r"), xor_pairs(count, slot)) for slot in range(1, count)
    ]
    return trade(jnp.concatenate(xor_order(parts, index), 0)).astype(FULL)


def spread_bits(turn):
    bits = []
    bit = 1
    while bit < lax.axis_size("q"):
        bits.append(bit)
        bit *= 2
    return bits[::-1] if turn else bits


def spread_places(bits):
    masks = [0]
    for bit in bits:
        masks = masks + [mask ^ bit for mask in masks]
    return lax.axis_index("q") ^ jnp.array(masks, jnp.int32)


def away_pairs(bit):
    count = lax.axis_size("q")
    return [
        ((spot * 2 + core) * 2 + 1 - core, ((spot ^ bit) * 2 + core) * 2 + 1 - core)
        for spot in range(count)
        for core in range(2)
    ]


def double(stack, bits, names, pairs):
    for bit in bits:
        stack = jnp.concatenate([stack, lax.ppermute(stack, names, pairs(bit))], 0)
    return stack


def place_kernel(place_ref, home_ref, own_ref, stack_ref, out_ref):
    del place_ref

    @pl.when(home_ref[0] == 1)
    def _():
        out_ref[...] = own_ref[0]

    @pl.when(home_ref[0] == 0)
    def _():
        out_ref[...] = stack_ref[0]


def fetch_weight(weight, layer, turn):
    count = lax.axis_size("q")
    rows, width = weight.shape[1] // count, weight.shape[2]
    part = lax.dynamic_slice(
        weight, (layer, lax.axis_index("q") * rows, 0), (1, rows, width)
    )
    part = lax.ppermute(part, ("c", "h"), [(1, 2), (2, 1)])
    bits = spread_bits(turn)
    stack = double(part, bits, ("q", "c", "h"), away_pairs)
    return pl.pallas_call(
        place_kernel,
        name="place_weight",
        grid_spec=pltpu.PrefetchScalarGridSpec(
            num_scalar_prefetch=2,
            grid=(count,),
            in_specs=[
                pl.BlockSpec((1, rows, width), lambda k, place, home: (layer, place[k], 0)),
                pl.BlockSpec((1, rows, width), lambda k, place, home: (k, 0, 0)),
            ],
            out_specs=pl.BlockSpec((rows, width), lambda k, place, home: (place[k], 0)),
        ),
        out_shape=jax.ShapeDtypeStruct(weight.shape[1:], weight.dtype),
        cost_estimate=pl.CostEstimate(
            flops=0, bytes_accessed=6 * count * rows * width, transcendentals=0
        ),
    )(spread_places(bits), is_home().astype(jnp.int32)[None], weight, stack)


def widen_kernel(place_ref, core_ref, own_ref, far_ref, *rest):
    del place_ref, core_ref
    out_ref = rest[-1]

    @pl.when(pl.program_id(0) == 0)
    def _():
        out_ref[0] = own_ref[0].astype(FULL)

    @pl.when(pl.program_id(0) == 1)
    def _():
        out_ref[0] = far_ref[0].astype(FULL)


def reduce_weight(gradient, layer, turn, target):
    count = lax.axis_size("q")
    spot = lax.axis_index("q")
    rows, width = gradient.shape
    bits = spread_bits(turn)
    natural = spread_bits(False)[::-1]
    part = gradient.reshape((2,) * len(bits) + (rows // count, width))
    names = list(natural)
    for bit in bits[::-1]:
        mine = (spot // bit) % 2
        axis = names.index(bit)
        names.pop(axis)
        kept = lax.dynamic_index_in_dim(part, mine, axis, keepdims=False)
        sent = lax.dynamic_index_in_dim(part, 1 - mine, axis, keepdims=False)
        sent = lax.ppermute(sent, "q", xor_pairs(count, bit))
        part = (kept.astype(FULL) + sent.astype(FULL)).astype(HALF)
    part = trade(part)
    core = lax.axis_index("c")
    part = part.reshape(2, rows // count // 2, width)
    kept = lax.dynamic_index_in_dim(part, core, 0)
    sent = other_core(lax.dynamic_index_in_dim(part, 1 - core, 0))
    total = (kept.astype(FULL) + sent.astype(FULL)).astype(HALF)
    stack = double(total, bits, "q", lambda bit: xor_pairs(count, bit))
    far = other_core(stack)
    part_rows = rows // count // 2
    operands = [spread_places(bits), core.astype(jnp.int32)[None], stack, far]
    in_specs = [
        pl.BlockSpec(
            (1, part_rows, width), lambda e, k, place, core: (jnp.where(e == 0, k, count - 1), 0, 0)
        ),
        pl.BlockSpec((1, part_rows, width), lambda e, k, place, core: (jnp.where(e == 1, k, 0), 0, 0)),
    ]
    aliases = {}
    if target is not None:
        operands.append(target)
        in_specs.append(pl.BlockSpec(memory_space=pl.ANY))
        aliases = {4: 0}
    return pl.pallas_call(
        widen_kernel,
        name="widen_gradient",
        grid_spec=pltpu.PrefetchScalarGridSpec(
            num_scalar_prefetch=2,
            grid=(2, count),
            in_specs=in_specs,
            out_specs=pl.BlockSpec(
                (1, part_rows, width),
                lambda e, k, place, core: (layer, place[k] * 2 + (core[0] ^ e), 0),
            ),
        ),
        out_shape=jax.ShapeDtypeStruct((LAYERS, rows, width), FULL),
        input_output_aliases=aliases,
        cost_estimate=pl.CostEstimate(
            flops=0, bytes_accessed=6 * rows * width, transcendentals=0
        ),
    )(*operands)


def sum_over(block, name):
    count = lax.axis_size(name)
    bit = 1
    while bit < count:
        block = block + lax.ppermute(block, name, xor_pairs(count, bit))
        bit *= 2
    return block


def norm_forward(stream, gain, bias):
    centred = stream - jnp.mean(stream, 1, keepdims=True)
    reciprocal = lax.rsqrt(jnp.mean(centred * centred, 1, keepdims=True) + EPS)
    normed = centred * reciprocal
    return ((normed * gain + bias).astype(HALF), normed, reciprocal)


def norm_backward(grad_normed, normed, reciprocal, gain):
    scaled = grad_normed * gain
    result = reciprocal * (
        scaled
        - jnp.mean(scaled, 1, keepdims=True)
        - normed * jnp.mean(scaled * normed, 1, keepdims=True)
    )
    return (result, jnp.sum(grad_normed * normed, 0), jnp.sum(grad_normed, 0))


def shards(
    tokens,
    first_gain,
    first_bias,
    triple_weight,
    query_bias,
    value_bias,
    output_weight,
    output_bias,
    second_gain,
    second_bias,
    up_weight,
    up_bias,
    down_weight,
    down_bias,
    cotangent,
):
    length = tokens.shape[0]
    group = 2 * lax.axis_size("r")
    block = length // group
    local_heads = query_bias.shape[1] // HEAD
    index = group_index()
    head_ids = (index * local_heads + jnp.arange(local_heads)).astype(FULL)
    slopes = jnp.exp2(-8.0 * (head_ids + 1.0) / (local_heads * group))
    local = jnp.arange(length)
    place = ((local // block) ^ index) * block + local % block
    place = place.astype(FULL)

    token_rows = enter(tokens)
    shift = trade(jnp.concatenate([query_bias, value_bias, up_bias], 1))
    width = local_heads * HEAD
    query_bias, value_bias, up_bias = (
        shift[:, :width],
        shift[:, width : 2 * width],
        shift[:, 2 * width :],
    )
    weights = []
    for layer in range(LAYERS):
        weights.append(
            [
                fetch_weight(member, layer, turn)
                for member, turn in (
                    (triple_weight, 0),
                    (output_weight, 1),
                    (up_weight, 1),
                    (down_weight, 0),
                )
            ]
        )
    cotangent_rows = enter(cotangent)

    stream = token_rows[:block].astype(FULL)
    saved = []
    for layer in range(LAYERS):
        triple, output, up, down = weights[layer]
        gain, bias = first_gain[layer], first_bias[layer]
        own_rows, first_normed, first_recip = norm_forward(stream, gain, bias)
        if layer == 0:
            first_rows = norm_forward(token_rows.astype(FULL), gain, bias)[0]
        else:
            first_rows = gather_rows(own_rows)
        joined_bias = jnp.stack(
            [
                query_bias[layer].reshape(local_heads, HEAD),
                jnp.zeros((local_heads, HEAD), FULL),
                value_bias[layer].reshape(local_heads, HEAD),
            ],
            1,
        ).reshape(1, 3 * width)
        joined = (dot(first_rows, triple, 1, 0) + joined_bias).astype(HALF)
        context = attend_forward(joined, slopes, place)
        branch = scatter_rows(dot(context, output, 1, 0).astype(HALF))
        stream = stream + (branch + output_bias[layer])
        own_rows, second_normed, second_recip = norm_forward(
            stream, second_gain[layer], second_bias[layer]
        )
        second_rows = gather_rows(own_rows)
        pre_act = dot(second_rows, up, 1, 0) + up_bias[layer]
        hidden = activate(pre_act).astype(HALF)
        branch = scatter_rows(dot(hidden, down, 1, 0).astype(HALF))
        stream = stream + (branch + down_bias[layer])
        saved.append(
            (
                first_rows,
                first_normed,
                first_recip,
                joined,
                context,
                second_rows,
                second_normed,
                second_recip,
                pre_act,
                hidden,
            )
        )
    block_out = leave(stream)

    gradient = cotangent_rows[:block].astype(FULL)
    grad_rows = cotangent_rows
    grad_weights = [None] * 4
    minors = [None] * LAYERS
    shifts = [None] * LAYERS
    for layer in reversed(range(LAYERS)):
        triple, output, up, down = weights[layer]
        (
            first_rows,
            first_normed,
            first_recip,
            joined,
            context,
            second_rows,
            second_normed,
            second_recip,
            pre_act,
            hidden,
        ) = saved[layer]
        grad_down_bias = jnp.sum(gradient, 0)
        grad_weights[3] = reduce_weight(
            dot(hidden, grad_rows, 0, 0).astype(HALF), layer, 0, grad_weights[3]
        )
        grad_pre = activate_grad(pre_act, dot(grad_rows, down, 1, 1))
        pre_half = grad_pre.astype(HALF)
        grad_up_bias = jnp.sum(grad_pre, 0)
        grad_second = scatter_rows(dot(pre_half, up, 1, 1).astype(HALF))
        grad_weights[2] = reduce_weight(
            dot(second_rows, pre_half, 0, 0).astype(HALF), layer, 1, grad_weights[2]
        )
        step_grad, grad_second_gain, grad_second_bias = norm_backward(
            grad_second, second_normed, second_recip, second_gain[layer]
        )
        gradient = gradient + step_grad
        grad_output_bias = jnp.sum(gradient, 0)
        grad_rows = gather_rows(gradient.astype(HALF))
        grad_context = dot(grad_rows, output, 1, 1).astype(HALF)
        grad_joined, grad_shift = attend_backward(joined, grad_context, slopes, place)
        grad_first = scatter_rows(dot(grad_joined, triple, 1, 1).astype(HALF))
        grad_weights[1] = reduce_weight(
            dot(context, grad_rows, 0, 0).astype(HALF), layer, 1, grad_weights[1]
        )
        grad_weights[0] = reduce_weight(
            dot(first_rows, grad_joined, 0, 0).astype(HALF), layer, 0, grad_weights[0]
        )
        step_grad, grad_first_gain, grad_first_bias = norm_backward(
            grad_first, first_normed, first_recip, first_gain[layer]
        )
        gradient = gradient + step_grad
        if layer > 0:
            grad_rows = gather_rows(gradient.astype(HALF))
        grad_shift = grad_shift.reshape(local_heads, 3, HEAD)
        shifts[layer] = jnp.concatenate(
            [grad_shift[:, 0].reshape(width), grad_shift[:, 2].reshape(width), grad_up_bias]
        )
        minors[layer] = jnp.stack(
            [
                grad_first_gain,
                grad_first_bias,
                grad_output_bias,
                grad_second_gain,
                grad_second_bias,
                grad_down_bias,
            ]
        )
    grad_tokens = leave(gradient)

    small = sum_over(jnp.stack(minors), "q")
    for name in ("r", "h", "c"):
        small = sum_over(small, name)
    shift = sum_over(trade(sum_over(jnp.stack(shifts), "q")), "c")
    stacked = grad_weights
    return (
        block_out,
        grad_tokens,
        small[:, 0],
        small[:, 1],
        stacked[0],
        shift[:, :width],
        shift[:, width : 2 * width],
        stacked[1],
        small[:, 2],
        small[:, 3],
        small[:, 4],
        stacked[2],
        shift[:, 2 * width :],
        stacked[3],
        small[:, 5],
    )


def solution(mesh):
    data, tensor = mesh.shape["dp"], mesh.shape["tensor"]
    fine = Mesh(mesh.devices.reshape(data // 2, 2, 2, tensor // 2), ("q", "c", "h", "r"))
    rows, cols = ("q", "c"), ("h", "r")
    in_specs = (
        P(rows, cols),
        P(),
        P(),
        P(None, None, cols),
        P(None, cols),
        P(None, cols),
        P(None, cols, None),
        P(),
        P(),
        P(),
        P(None, None, cols),
        P(None, cols),
        P(None, cols, None),
        P(),
        P(rows, cols),
    )
    out_specs = (
        P(rows, cols),
        P(rows, cols),
        P(),
        P(),
        P(None, None, cols),
        P(None, cols),
        P(None, cols),
        P(None, cols, None),
        P(),
        P(),
        P(),
        P(None, None, cols),
        P(None, cols),
        P(None, cols, None),
        P(),
    )
    return jax.shard_map(shards, mesh=fine, in_specs=in_specs, out_specs=out_specs, check_vma=False)
```

```python
import functools

import jax
import jax.numpy as jnp
from jax import lax
from jax.experimental import pallas as pl
from jax.experimental.pallas import tpu as pltpu
from jax.sharding import Mesh, PartitionSpec as P


HEAD = 64
LAYERS = 2

EPS = 1e-05
CUBIC = 0.044715
ROOT = 0.7978845608028654
LOW = -1e30

HALF = jnp.bfloat16
FULL = jnp.float32


def activate(inputs):
    return 0.5 * inputs * (1.0 + jnp.tanh(ROOT * (inputs + CUBIC * inputs * inputs * inputs)))


def activate_grad(inputs, upstream):
    return jax.vjp(activate, inputs)[1](upstream)[0]


def dot(former, latter, former_dim, latter_dim):
    return lax.dot_general(
        former, latter, (((former_dim,), (latter_dim,)), ((), ())), preferred_element_type=FULL
    )


def softmax_rows(queries, key_part, slope, distance):
    scores = dot(queries, key_part, 1, 1) * HEAD ** (-0.5) - slope * distance
    scores = jnp.where(distance >= 0, scores, LOW)
    raised = jnp.exp(scores - jnp.max(scores, -1, keepdims=True))
    return raised * (1.0 / jnp.sum(raised, -1, keepdims=True))


def forward_kernel(pieces, slope_ref, column_ref, row_ref, joined_ref, context_ref):
    length = joined_ref.shape[0]
    rows = length // pieces
    pair = pl.program_id(0)
    for member in range(2):
        slope = slope_ref[2 * pair + member]
        start = member * 3 * HEAD
        key_part = joined_ref[:, start + HEAD : start + 2 * HEAD]
        values = joined_ref[:, start + 2 * HEAD : start + 3 * HEAD]
        for piece in range(pieces):
            span = slice(piece * rows, (piece + 1) * rows)
            distance = column_ref[span, :] - row_ref[...]
            attention = softmax_rows(
                joined_ref[span, start : start + HEAD], key_part, slope, distance
            )
            context = dot(attention.astype(HALF), values, 1, 0)
            context_ref[span, member * HEAD : (member + 1) * HEAD] = context.astype(HALF)


def backward_kernel(
    pieces,
    slope_ref,
    column_ref,
    row_ref,
    joined_ref,
    context_ref,
    grad_ref,
    total_ref,
    key_ref,
    value_ref,
):
    length = joined_ref.shape[0]
    rows = length // pieces
    pair = pl.program_id(0)
    for member in range(2):
        slope = slope_ref[2 * pair + member]
        start = member * 3 * HEAD
        key_part = joined_ref[:, start + HEAD : start + 2 * HEAD]
        values = joined_ref[:, start + 2 * HEAD : start + 3 * HEAD]
        query_total = jnp.zeros((1, HEAD), FULL)
        for piece in range(pieces):
            span = slice(piece * rows, (piece + 1) * rows)
            distance = column_ref[span, :] - row_ref[...]
            queries = joined_ref[span, start : start + HEAD]
            upstream = context_ref[span, member * HEAD : (member + 1) * HEAD]
            attention = softmax_rows(queries, key_part, slope, distance)
            grad_values = dot(attention.astype(HALF), upstream, 0, 0)
            grad_attention = dot(upstream, values, 1, 1)
            weighted = attention * grad_attention
            grad_scores = weighted - attention * jnp.sum(weighted, -1, keepdims=True)
            score_half = (grad_scores * HEAD ** (-0.5)).astype(HALF)
            grad_queries = dot(score_half, key_part, 1, 0)
            grad_keys = dot(score_half, queries, 0, 0)
            grad_ref[span, start : start + HEAD] = grad_queries.astype(HALF)
            query_total = query_total + jnp.sum(grad_queries, 0, keepdims=True)
            if piece == 0:
                key_ref[...] = grad_keys
                value_ref[...] = grad_values
            else:
                key_ref[...] += grad_keys
                value_ref[...] += grad_values
        grad_ref[:, start + HEAD : start + 2 * HEAD] = key_ref[...].astype(HALF)
        grad_ref[:, start + 2 * HEAD : start + 3 * HEAD] = value_ref[...].astype(HALF)
        eight = (8, HEAD)
        total_ref[0, :, start : start + HEAD] = jnp.broadcast_to(query_total, eight)
        total_ref[0, :, start + HEAD : start + 2 * HEAD] = jnp.zeros(eight, FULL)
        total_ref[0, :, start + 2 * HEAD : start + 3 * HEAD] = jnp.broadcast_to(
            jnp.sum(value_ref[...], 0, keepdims=True), eight
        )


def attention_specs(length):
    return [
        pl.BlockSpec(memory_space=pltpu.SMEM),
        pl.BlockSpec((length, 1), lambda pair: (0, 0)),
        pl.BlockSpec((1, length), lambda pair: (0, 0)),
        pl.BlockSpec((length, 6 * HEAD), lambda pair: (0, pair)),
    ]


def attend_forward(joined, slopes, place):
    length, width = joined.shape
    pairs = width // (6 * HEAD)
    return pl.pallas_call(
        functools.partial(forward_kernel, 4),
        name="af",
        grid=(pairs,),
        in_specs=attention_specs(length),
        out_specs=pl.BlockSpec((length, 2 * HEAD), lambda pair: (0, pair)),
        out_shape=jax.ShapeDtypeStruct((length, pairs * 2 * HEAD), HALF),
        cost_estimate=pl.CostEstimate(
            flops=pairs * 2 * 4 * length * length * HEAD,
            bytes_accessed=length * width * 3,
            transcendentals=pairs * 2 * length * length,
        ),
    )(slopes, place[:, None], place[None, :], joined)


def attend_backward(joined, grad_context, slopes, place):
    length, width = joined.shape
    pairs = width // (6 * HEAD)
    grad_joined, totals = pl.pallas_call(
        functools.partial(backward_kernel, 4),
        name="ak",
        grid=(pairs,),
        in_specs=attention_specs(length)
        + [pl.BlockSpec((length, 2 * HEAD), lambda pair: (0, pair))],
        out_specs=[
            pl.BlockSpec((length, 6 * HEAD), lambda pair: (0, pair)),
            pl.BlockSpec((1, 8, 6 * HEAD), lambda pair: (pair, 0, 0)),
        ],
        out_shape=[
            jax.ShapeDtypeStruct((length, width), HALF),
            jax.ShapeDtypeStruct((pairs, 8, 6 * HEAD), FULL),
        ],
        scratch_shapes=[pltpu.VMEM((length, HEAD), FULL), pltpu.VMEM((length, HEAD), FULL)],
        cost_estimate=pl.CostEstimate(
            flops=pairs * 2 * 10 * length * length * HEAD,
            bytes_accessed=length * width * 5,
            transcendentals=pairs * 2 * length * length,
        ),
    )(slopes, place[:, None], place[None, :], joined, grad_context)
    return grad_joined, totals[:, 0].reshape(width)


def xor_pairs(count, bit):
    return [(source, source ^ bit) for source in range(count)]


def other_core(block):
    return lax.ppermute(block, "c", [(0, 1), (1, 0)])


def is_home():
    return lax.axis_index("c") == lax.axis_index("h")


def trade(block):
    received = lax.ppermute(block, ("c", "h"), [(1, 2), (2, 1)])
    return jnp.where(is_home(), block, received)


def group_index():
    return lax.axis_index("c") * lax.axis_size("r") + lax.axis_index("r")


def xor_order(blocks, index):
    bit = 1
    while bit < len(blocks):
        flip = (index // bit) % 2 == 1
        blocks = [
            jnp.where(flip, blocks[slot ^ bit], blocks[slot]) for slot in range(len(blocks))
        ]
        bit *= 2
    return blocks


def gather_list(own):
    ring = lax.axis_size("r")
    near = {0: own}
    bit = 1
    while bit < ring:
        for slot in list(near):
            near[slot ^ bit] = lax.ppermute(near[slot], "r", xor_pairs(ring, bit))
        bit *= 2
    near = [near[slot] for slot in range(ring)]
    return near + [other_core(block) for block in near]


def gather_rows(own):
    return jnp.concatenate(gather_list(own), 0)


def scatter_rows(partial_value):
    ring = lax.axis_size("r")
    half = partial_value.shape[0] // 2
    block = half // ring
    total = partial_value[:half].astype(FULL) + other_core(partial_value[half:]).astype(FULL)
    count = ring
    while count > 1:
        bit = count // 2
        sent = lax.ppermute(
            total[bit * block :].astype(HALF), "r", xor_pairs(ring, bit)
        )
        total = total[: bit * block] + sent.astype(FULL)
        count = bit
    return total


def enter(shard):
    index = group_index()
    block = trade(shard)
    blocks = gather_list(block)
    full = jnp.concatenate(xor_order(blocks, index), 1)
    count = len(blocks)
    rows = full.shape[0] // count
    parts = [full[slot * rows : (slot + 1) * rows] for slot in range(count)]
    return jnp.concatenate(xor_order(parts, index), 0)


def leave(own):
    index = group_index()
    count = 2 * lax.axis_size("r")
    width = own.shape[1] // count
    own = own.astype(HALF)
    parts = xor_order([own[:, slot * width : (slot + 1) * width] for slot in range(count)], index)
    parts = [parts[0]] + [
        lax.ppermute(parts[slot], ("c", "r"), xor_pairs(count, slot))
        for slot in range(1, count)
    ]
    full = jnp.concatenate(xor_order(parts, index), 0)
    return trade(full).astype(FULL)


def spread_bits(turn):
    bits = []
    bit = 1
    while bit < lax.axis_size("q"):
        bits.append(bit)
        bit *= 2
    return bits[::-1] if turn else bits


def spread_places(bits):
    masks = [0]
    for bit in bits:
        masks = masks + [mask ^ bit for mask in masks]
    return lax.axis_index("q") ^ jnp.array(masks, jnp.int32)


def away_pairs(bit):
    count = lax.axis_size("q")
    return [
        ((spot * 2 + core) * 2 + 1 - core, ((spot ^ bit) * 2 + core) * 2 + 1 - core)
        for spot in range(count)
        for core in range(2)
    ]


def double(stack, bits, names, pairs):
    for bit in bits:
        stack = jnp.concatenate([stack, lax.ppermute(stack, names, pairs(bit))], 0)
    return stack


def after(block, earlier):
    return lax.optimization_barrier((block, earlier))[0]


def place_kernel(place_ref, home_ref, own_ref, *rest):
    pieces, out_ref = rest[:-1], rest[-1]

    @pl.when(home_ref[0] == 1)
    def _():
        out_ref[...] = own_ref[0]

    @pl.when(home_ref[0] == 0)
    def _():
        for step, piece_ref in enumerate(pieces):
            out_ref[place_ref[step]] = piece_ref[...]


def column_parts(width):
    return 2 if width % 256 == 0 else 1


def own_part(weight, layer):
    rows = weight.shape[1] // lax.axis_size("q")
    return lax.dynamic_slice(
        weight, (layer, lax.axis_index("q") * rows, 0), (1, rows, weight.shape[2])
    )[0]


def cross(part):
    return lax.ppermute(part, ("c", "h"), [(1, 2), (2, 1)])


def merge_parts(pieces, width):
    return jnp.concatenate([piece.reshape(-1, width) for piece in pieces], 0)


def split_parts(merged, shapes):
    pieces, start = [], 0
    for rows, width in shapes:
        count = rows * width // merged.shape[1]
        pieces.append(merged[start : start + count].reshape(rows, width))
        start += count
    return pieces


def fetch_placed(weight, layer, pieces, start):
    count = lax.axis_size("q")
    rows, width = weight.shape[1] // count, weight.shape[2]
    if width != pieces[0].shape[1] or start % rows:
        size = rows * width // pieces[0].shape[1]
        pieces = [piece[start : start + size].reshape(rows, width) for piece in pieces]
        start = 0
    home = is_home().astype(jnp.int32)[None]
    offset = start // rows
    columns = column_parts(width)
    part = width // columns
    return pl.pallas_call(
        place_kernel,
        name="pw",
        grid_spec=pltpu.PrefetchScalarGridSpec(
            num_scalar_prefetch=2,
            grid=(columns,),
            in_specs=[
                pl.BlockSpec((1, count, rows, part), lambda j, place, home: (layer, 0, 0, j))
            ]
            + [pl.BlockSpec((rows, part), lambda j, place, home: (offset, j))] * count,
            out_specs=pl.BlockSpec((count, rows, part), lambda j, place, home: (0, 0, j)),
        ),
        out_shape=jax.ShapeDtypeStruct((count, rows, width), weight.dtype),
        cost_estimate=pl.CostEstimate(
            flops=0, bytes_accessed=6 * count * rows * width, transcendentals=0
        ),
    )(
        spread_places(spread_bits(False)),
        home,
        weight.reshape(LAYERS, count, rows, width),
        *pieces,
    ).reshape(weight.shape[1:])


def widen_kernel(place_ref, core_ref, own_ref, far_ref, *rest):
    out_ref = rest[-1]
    core = core_ref[0]
    for step in range(own_ref.shape[0]):
        out_ref[0, place_ref[step], core] = own_ref[step].astype(FULL)
        out_ref[0, place_ref[step], 1 - core] = far_ref[step].astype(FULL)


def widen_plain_kernel(own_ref, *rest):
    rest[-1][0] = own_ref[...].astype(FULL)


def core_halves(pieces, width):
    core = lax.axis_index("c")
    shaped = [piece.reshape(2, piece.shape[0] // 2, piece.shape[1]) for piece in pieces]
    kept = [lax.dynamic_index_in_dim(piece, core, 0, keepdims=False) for piece in shaped]
    sent = [lax.dynamic_index_in_dim(piece, 1 - core, 0, keepdims=False) for piece in shaped]
    got = split_parts(other_core(merge_parts(sent, width)), [piece.shape for piece in kept])
    return [
        (mine.astype(FULL) + other.astype(FULL)).astype(HALF)
        for mine, other in zip(kept, got, strict=True)
    ]


def widen_plain(total, start, rows, width, layer, target):
    count = total.shape[0]
    block = rows // count
    if width != total.shape[2] or start % block:
        size = block * width // total.shape[2]
        total = total[:, start : start + size].reshape(count, block, width)
        start = 0
    offset = start // block
    operands, aliases = [total], {}
    shape = (LAYERS, count, block, width)
    in_specs = [pl.BlockSpec((count // 2, block, width), lambda k: (k, offset, 0))]
    if target is not None:
        operands.append(target.reshape(shape))
        in_specs.append(pl.BlockSpec(memory_space=pl.ANY))
        aliases = {1: 0}
    return pl.pallas_call(
        widen_plain_kernel,
        name="wp",
        grid=(2,),
        in_specs=in_specs,
        out_specs=pl.BlockSpec((1, count // 2, block, width), lambda k: (layer, k, 0, 0)),
        out_shape=jax.ShapeDtypeStruct(shape, FULL),
        input_output_aliases=aliases,
        cost_estimate=pl.CostEstimate(
            flops=0, bytes_accessed=6 * rows * width, transcendentals=0
        ),
    )(*operands).reshape(LAYERS, rows, width)


def reduce_placed(gradients, turn):
    count = lax.axis_size("q")
    spot = lax.axis_index("q")
    width = gradients[0].shape[1]
    bits = spread_bits(turn)
    names = spread_bits(True)
    sizes = [gradient.shape[0] // count for gradient in gradients]
    cube = (2,) * len(bits)
    part = jnp.concatenate(
        [
            gradient.reshape(cube + (size, width))
            for gradient, size in zip(gradients, sizes, strict=True)
        ],
        len(bits),
    )
    for bit in bits[::-1]:
        mine = (spot // bit) % 2
        axis = names.index(bit)
        names.pop(axis)
        kept = lax.dynamic_index_in_dim(part, mine, axis, keepdims=False)
        sent = lax.dynamic_index_in_dim(part, 1 - mine, axis, keepdims=False)
        sent = lax.ppermute(sent, "q", xor_pairs(count, bit))
        part = (kept.astype(FULL) + sent.astype(FULL)).astype(HALF)
    part = trade(part)
    pieces = core_halves(split_parts(part, [(size, width) for size in sizes]), width)
    stack = double(
        jnp.concatenate(pieces, 0)[None], bits, "q", lambda bit: xor_pairs(count, bit)
    )
    return stack, other_core(stack), turn


def widen_placed(parts, start, rows, layer, target):
    stack, far, turn = parts
    count, _, width = stack.shape
    block = rows // (2 * count)
    columns = column_parts(width)
    offset = start // block
    shape = (LAYERS, count, 2, block, width)
    operands = [
        spread_places(spread_bits(turn)),
        lax.axis_index("c").astype(jnp.int32)[None],
        stack,
        far,
    ]
    in_specs = [
        pl.BlockSpec((count, block, width // columns), lambda j, place, core: (0, offset, j))
    ] * 2
    aliases = {}
    if target is not None:
        operands.append(target.reshape(shape))
        in_specs.append(pl.BlockSpec(memory_space=pl.ANY))
        aliases = {4: 0}
    return pl.pallas_call(
        widen_kernel,
        name="wd",
        grid_spec=pltpu.PrefetchScalarGridSpec(
            num_scalar_prefetch=2,
            grid=(columns,),
            in_specs=in_specs,
            out_specs=pl.BlockSpec(
                (1, count, 2, block, width // columns),
                lambda j, place, core: (layer, 0, 0, 0, j),
            ),
        ),
        out_shape=jax.ShapeDtypeStruct(shape, FULL),
        input_output_aliases=aliases,
        cost_estimate=pl.CostEstimate(
            flops=0, bytes_accessed=6 * rows * width, transcendentals=0
        ),
    )(*operands).reshape(LAYERS, rows, width)


def sum_over(block, name):
    count = lax.axis_size(name)
    bit = 1
    while bit < count:
        block = block + lax.ppermute(block, name, xor_pairs(count, bit))
        bit *= 2
    return block


def norm_forward(stream, gain, bias):
    centred = stream - jnp.mean(stream, 1, keepdims=True)
    reciprocal = lax.rsqrt(jnp.mean(centred * centred, 1, keepdims=True) + EPS)
    normed = centred * reciprocal
    return ((normed * gain + bias).astype(HALF), normed, reciprocal)


def norm_backward(grad_normed, normed, reciprocal, gain):
    scaled = grad_normed * gain
    result = reciprocal * (
        scaled
        - jnp.mean(scaled, 1, keepdims=True)
        - normed * jnp.mean(scaled * normed, 1, keepdims=True)
    )
    return (result, jnp.sum(grad_normed * normed, 0), jnp.sum(grad_normed, 0))


def run(
    tokens,
    first_gain,
    first_bias,
    triple_weight,
    query_bias,
    value_bias,
    output_weight,
    output_bias,
    second_gain,
    second_bias,
    up_weight,
    up_bias,
    down_weight,
    down_bias,
    cotangent,
):
    length = tokens.shape[0]
    group = 2 * lax.axis_size("r")
    block = length // group
    local_heads = query_bias.shape[1] // HEAD
    index = group_index()
    head_ids = (index * local_heads + jnp.arange(local_heads)).astype(FULL)
    slopes = jnp.exp2(-8.0 * (head_ids + 1.0) / (local_heads * group))
    local = jnp.arange(length)
    place = ((local // block) ^ index) * block + local % block
    place = place.astype(FULL)

    model = second_gain.shape[1]
    spread = lax.axis_size("q")
    others = (up_weight, down_weight, output_weight)
    shapes = [(member.shape[1] // spread, member.shape[2]) for member in others]
    merged = [
        merge_parts([own_part(member, 0) for member in others], model),
        merge_parts([own_part(member, 1) for member in (down_weight, up_weight, output_weight)], model),
    ]
    sizes = [rows * width // model for rows, width in shapes]
    triples = [own_part(triple_weight, layer) for layer in range(LAYERS)]
    got_triple = cross(triples[0])
    token_rows = enter(tokens)
    got = cross(merged[0])
    later = merge_parts([merged[1], triples[1]], model)
    got_later = cross(after(later, got))
    shift = trade(jnp.concatenate([query_bias, value_bias, up_bias], 1))
    width = local_heads * HEAD
    query_bias, value_bias, up_bias = (
        shift[:, :width],
        shift[:, width : 2 * width],
        shift[:, 2 * width :],
    )
    triple = lax.all_gather(
        jnp.where(is_home(), triples[0], got_triple), "q", axis=0, tiled=True
    )
    pieces = [got]
    for step in range(1, spread):
        pieces.append(lax.ppermute(got, ("q", "c", "h"), away_pairs(step)))
    weights = [
        [
            triple,
            fetch_placed(output_weight, 0, pieces, sizes[0] + sizes[1]),
            fetch_placed(up_weight, 0, pieces, 0),
            fetch_placed(down_weight, 0, pieces, sizes[0]),
        ]
    ]
    total = sum(sizes)
    part = jnp.where(is_home(), triples[1], got_later[total:].reshape(triples[1].shape))
    triple = lax.all_gather(part, "q", axis=0, tiled=True)
    part = jnp.where(is_home(), merged[1], got_later[:total])
    size = sizes[1]
    rest = lax.all_gather(part[None, size:], "q", axis=0, tiled=True)
    up = rest[:, : sizes[0]].reshape(up_weight.shape[1:])
    output = rest[:, sizes[0] :].reshape(output_weight.shape[1:])
    down = lax.all_gather(part[:size], "q", axis=0, tiled=True)
    weights.append([triple, output, up, down])
    cotangent_rows = enter(after(cotangent, got))

    stream = token_rows[:block].astype(FULL)
    saved = []
    for layer in range(LAYERS):
        triple, output, up, down = weights[layer]
        gain, bias = first_gain[layer], first_bias[layer]
        own_rows, first_normed, first_recip = norm_forward(stream, gain, bias)
        if layer == 0:
            first_rows = norm_forward(token_rows.astype(FULL), gain, bias)[0]
        else:
            first_rows = gather_rows(own_rows)
        joined_bias = jnp.stack(
            [
                query_bias[layer].reshape(local_heads, HEAD),
                jnp.zeros((local_heads, HEAD), FULL),
                value_bias[layer].reshape(local_heads, HEAD),
            ],
            1,
        ).reshape(1, 3 * width)
        joined = (dot(first_rows, triple, 1, 0) + joined_bias).astype(HALF)
        context = attend_forward(joined, slopes, place)
        branch = dot(context, output, 1, 0).astype(HALF)
        branch = scatter_rows(branch)
        stream = stream + (branch + output_bias[layer])
        own_rows, second_normed, second_recip = norm_forward(
            stream, second_gain[layer], second_bias[layer]
        )
        second_rows = gather_rows(own_rows)
        pre_act = dot(second_rows, up, 1, 0) + up_bias[layer]
        hidden = activate(pre_act).astype(HALF)
        branch = scatter_rows(dot(hidden, down, 1, 0).astype(HALF))
        stream = stream + (branch + down_bias[layer])
        saved.append(
            (
                first_rows,
                first_normed,
                first_recip,
                joined,
                context,
                second_rows,
                second_normed,
                second_recip,
                pre_act,
                hidden,
            )
        )
    block_out = leave(stream)

    gradient = cotangent_rows[:block].astype(FULL)
    grad_rows = cotangent_rows
    waiting = {}
    minors = [None] * LAYERS
    shifts = [None] * LAYERS
    for layer in reversed(range(LAYERS)):
        triple, output, up, down = weights[layer]
        (
            first_rows,
            first_normed,
            first_recip,
            joined,
            context,
            second_rows,
            second_normed,
            second_recip,
            pre_act,
            hidden,
        ) = saved[layer]
        grad_down_bias = jnp.sum(gradient, 0)
        raw_down = dot(hidden, grad_rows, 0, 0).astype(HALF)
        grad_pre = activate_grad(pre_act, dot(grad_rows, down, 1, 1))
        pre_half = grad_pre.astype(HALF)
        grad_up_bias = jnp.sum(grad_pre, 0)
        grad_second = scatter_rows(dot(pre_half, up, 1, 1).astype(HALF))
        raw_up = dot(second_rows, pre_half, 0, 0).astype(HALF)
        step_grad, grad_second_gain, grad_second_bias = norm_backward(
            grad_second, second_normed, second_recip, second_gain[layer]
        )
        gradient = gradient + step_grad
        grad_output_bias = jnp.sum(gradient, 0)
        grad_rows = after(gather_rows(gradient.astype(HALF)), (raw_down, raw_up))
        raw_output = dot(context, grad_rows, 0, 0).astype(HALF)
        if layer > 0:
            waiting["n"] = lax.psum_scatter(raw_down, "q", scatter_dimension=0, tiled=True)
            waiting["up"] = lax.psum_scatter(raw_up, "q", scatter_dimension=0, tiled=True)
            waiting["o"] = raw_output
        else:
            ready = [waiting["n"], waiting["up"]]
            part = trade(after(merge_parts(ready, model), grad_rows))
            ready = core_halves(split_parts(part, [piece.shape for piece in ready]), model)
            rest = merge_parts(ready, model)[None]
            wide_rest = lax.all_gather(rest, ("q", "c"), axis=0, tiled=True)
            waiting["up"] = lax.psum_scatter(raw_up, "q", scatter_dimension=0, tiled=True)
            ring_rest = reduce_placed([raw_down, raw_output, waiting["o"]], 0)
        grad_context = dot(grad_rows, output, 1, 1).astype(HALF)
        grad_joined, grad_shift = attend_backward(joined, grad_context, slopes, place)
        grad_first = scatter_rows(dot(grad_joined, triple, 1, 1).astype(HALF))
        raw_triple = dot(first_rows, grad_joined, 0, 0).astype(HALF)
        step_grad, grad_first_gain, grad_first_bias = norm_backward(
            grad_first, first_normed, first_recip, first_gain[layer]
        )
        gradient = gradient + step_grad
        if layer > 0:
            grad_rows = after(gather_rows(gradient.astype(HALF)), (raw_triple, raw_output))
            waiting["x"] = lax.psum_scatter(
                raw_triple, "q", scatter_dimension=0, tiled=True
            )
        else:
            ring_triple = reduce_placed([raw_triple], 1)
            part = after(waiting["x"], raw_triple)
            part = trade(part)
            part = core_halves([part], part.shape[1])[0]
            wide_triple = lax.all_gather(part[None], ("q", "c"), axis=0, tiled=True)
            part = after(waiting["up"], raw_triple)
            part = trade(part)
            part = core_halves([part], model)
            wide_up = lax.all_gather(merge_parts(part, model)[None], ("q", "c"), axis=0, tiled=True)
        grad_shift = grad_shift.reshape(local_heads, 3, HEAD)
        shifts[layer] = jnp.concatenate(
            [grad_shift[:, 0].reshape(width), grad_shift[:, 2].reshape(width), grad_up_bias]
        )
        minors[layer] = jnp.stack(
            [
                grad_first_gain,
                grad_first_bias,
                grad_output_bias,
                grad_second_gain,
                grad_second_bias,
                grad_down_bias,
            ]
        )
    grad_tokens = leave(gradient)

    size = shifts[0].shape[0]
    slots = jnp.zeros((group, LAYERS, size), FULL)
    slots = lax.dynamic_update_slice(slots, jnp.stack(shifts)[None], (index, 0, 0))
    small = jnp.stack(minors)
    payload = jnp.concatenate([small.reshape(-1), slots.reshape(-1)]).reshape(-1, 128)
    payload = after(payload, gradient)
    for name in ("c", "q", "r", "h"):
        payload = sum_over(payload, name)
    payload = payload.reshape(-1)
    slots = payload[small.size :].reshape(group, LAYERS, size)
    small = payload[: small.size].reshape(small.shape)
    mine = lax.axis_index("h") * lax.axis_size("r") + lax.axis_index("r")
    shift = lax.dynamic_index_in_dim(slots, mine, 0, keepdims=False)

    rows_of = {
        "x": (model, triple_weight.shape[2]),
        "o": (output_weight.shape[1], model),
        "up": (model, up_weight.shape[2]),
        "n": (down_weight.shape[1], model),
    }
    parts = 2 * spread
    down_rows = rows_of["n"][0]
    output_rows = rows_of["o"][0]
    stacked = [None] * 4
    stacked[3] = widen_plain(wide_rest, 0, *rows_of["n"], 1, None)
    stacked[2] = widen_plain(wide_rest, down_rows // parts, *rows_of["up"], 1, None)
    stacked[0] = widen_plain(wide_triple, 0, *rows_of["x"], 1, None)
    stacked[3] = widen_placed(ring_rest, 0, down_rows, 0, stacked[3])
    stacked[1] = widen_placed(ring_rest, down_rows // parts, output_rows, 0, None)
    stacked[1] = widen_placed(
        ring_rest, (down_rows + output_rows) // parts, output_rows, 1, stacked[1]
    )
    stacked[0] = widen_placed(ring_triple, 0, model, 0, stacked[0])
    stacked[2] = widen_plain(wide_up, 0, *rows_of["up"], 0, stacked[2])
    return (
        block_out,
        grad_tokens,
        small[:, 0],
        small[:, 1],
        stacked[0],
        shift[:, :width],
        shift[:, width : 2 * width],
        stacked[1],
        small[:, 2],
        small[:, 3],
        small[:, 4],
        stacked[2],
        shift[:, 2 * width :],
        stacked[3],
        small[:, 5],
    )


def solution(mesh):
    data, tensor = mesh.shape["dp"], mesh.shape["tensor"]
    fine = Mesh(mesh.devices.reshape(data // 2, 2, 2, tensor // 2), ("q", "c", "h", "r"))
    rows, cols = ("q", "c"), ("h", "r")
    in_specs = (
        P(rows, cols),
        P(),
        P(),
        P(None, None, cols),
        P(None, cols),
        P(None, cols),
        P(None, cols, None),
        P(),
        P(),
        P(),
        P(None, None, cols),
        P(None, cols),
        P(None, cols, None),
        P(),
        P(rows, cols),
    )
    out_specs = (
        P(rows, cols),
        P(rows, cols),
        P(),
        P(),
        P(None, None, cols),
        P(None, cols),
        P(None, cols),
        P(None, cols, None),
        P(),
        P(),
        P(),
        P(None, None, cols),
        P(None, cols),
        P(None, cols, None),
        P(),
    )
    return jax.shard_map(run, mesh=fine, in_specs=in_specs, out_specs=out_specs, check_vma=False)
```
